1024 devices in a mesh: sub: 16 (over x, core), grp: 64 (over y, z).
Axes of the slice: x: 8, y: 8, z: 8, core: 2. Of those that a mesh axis runs over, the one named last changes fastest.
Arguments:
- load: float32 [64, 393216], P(None, ('sub', 'grp')), may hold values from -12 to 12
- visit_rows: int32 [1024, 768], P(('sub', 'grp')), may hold values from 0 to 383, as said below
- dual_ops: bfloat16 [1024, 768, 768], P(('sub', 'grp')), may hold values from -0.109375 to 0.109375
- dirichlet_ops: bfloat16 [1024, 768, 768], P(('sub', 'grp')), may hold values from -0.109375 to 0.109375
- coarse_maps: bfloat16 [1024, 24, 768], P(('sub', 'grp')), may hold values from -0.4375 to 0.4375
- primal: int32 [1024, 24], P(('sub', 'grp')), may hold values from 0 to 6143, as said below
- coarse_inverse: bfloat16 [6144, 6144], P('grp'), may hold values from -2 to 2
Outputs:
- multipliers: float32 [64, 393216], P(None, ('sub', 'grp'))
- residual: float32 [64, 393216], P(None, ('sub', 'grp'))
The draws below stay inside these ranges and needn't reach their ends.
Inputs may be any that keep to these rules, and one draw needn't show every extreme that they name: In every row of visit_rows each number from 0 to 383 appears exactly twice. The 24 entries of a row of primal are distinct, and every coarse row appears in exactly four rows of primal.
All inputs are finite; a program needn't handle non-finite values.
Results may differ from the reference program's by a relative error of at most 0.0088.
Values may be sent and summed in bfloat16 or wider, within the bound.
No kernel may reach another device: no remote copies, remote signals or barrier semaphores. Data moves between devices by JAX's collectives and lax.ppermute only.
A program may use at most 64 MiB of HBM per device.

```python
import jax
import jax.numpy as jnp
from jax import lax

M = 768
NP = 24
R = 64
ITERS = 2
SUBS = 1024
SLOT = 48
LAM = 384
NLAM = 393216
NC = 6144
N_SUB = 16
N_GRP = 64


def draw_visit_rows(key, part):
    keys = jax.random.split(jax.random.fold_in(key, 3), SUBS)
    orders = jax.vmap(lambda single: jax.random.permutation(single, M))(keys)
    return (orders // 2).astype(jnp.int32)


def draw_primal(key, part):
    ordinal = jnp.arange(SUBS, dtype=jnp.int32)
    sub_place = ordinal // N_GRP
    grp_place = ordinal % N_GRP
    corner = jnp.arange(8, dtype=jnp.int32)
    step_sub = corner // 4
    step_grp = corner // 2 % 2
    step_layer = corner % 2
    node_index = ((sub_place[:, None] + step_sub[None, :]) % N_SUB * N_GRP + (grp_place[:, None] + step_grp[None, :]) % N_GRP) * 2 + step_layer[None, :]
    dof_index = (node_index[:, :, None] * 3 + jnp.arange(3, dtype=jnp.int32)[None, None, :]).reshape(SUBS, NP)
    relabel = jax.random.permutation(jax.random.fold_in(key, 11), NC).astype(jnp.int32)
    keys = jax.random.split(jax.random.fold_in(key, 13), SUBS)
    orders = jax.vmap(lambda single: jax.random.permutation(single, NP))(keys).astype(jnp.int32)
    shuffled = jnp.take_along_axis(dof_index, orders, axis=1)
    labelled = jnp.take(relabel, shuffled).astype(jnp.int32)
    placement_order = jax.random.permutation(jax.random.fold_in(key, 17), SUBS).astype(jnp.int32)
    return jnp.take(labelled, placement_order, axis=0).astype(jnp.int32)


def draw_coarse_inverse(key, part):
    first, second = jax.random.split(jax.random.fold_in(key, 7))
    offdiag = jax.random.normal(first, (NC, NC), jnp.float32) * (0.3 * NC ** (-0.5))
    diagonal = jax.random.uniform(second, (NC,), jnp.float32, 0.5, 1.5)
    return (offdiag + jnp.diag(diagonal)).astype(jnp.bfloat16)


def level_of(stream_key, extent, cuts, low, high):
    factor_of = 1.0
    for dim, parts in cuts:
        draws = jax.random.uniform(jax.random.fold_in(jax.random.fold_in(stream_key, 6), dim), (parts,), jnp.float32, low / len(cuts), high / len(cuts))
        factor_of = factor_of * jnp.repeat(jnp.exp(draws), extent[dim] // parts).reshape((-1,) + (1,) * (len(extent) - 1 - dim))
    return factor_of


def centred(rng, dims, spread, most, cuts=(), kind=jnp.bfloat16):
    factor_of = level_of(rng, dims, cuts, -0.22, 0.18) if cuts else 1.0
    array = jax.random.normal(rng, dims, jnp.float32) * spread * factor_of
    return jnp.minimum(jnp.maximum(array, -most), most).astype(kind)


def setup_inputs(seed: int = 0) -> dict:
    key_list = jax.random.split(jax.random.key(seed), 8)
    return {
        "load": centred(key_list[0], (R, NLAM), 2.0, 12.0, ((1, 1024),), jnp.float32),
        "visit_rows": draw_visit_rows(jax.random.fold_in(key_list[7], 71), 0),
        "dual_ops": centred(key_list[2], (SUBS, M, M), (4 * M) ** -0.5, 0.109375, ((0, 1024),)),
        "dirichlet_ops": centred(key_list[3], (SUBS, M, M), (4 * M) ** -0.5, 0.109375, ((0, 1024),)),
        "coarse_maps": centred(key_list[4], (SUBS, NP, M), (M // 4) ** -0.5, 0.4375, ((0, 1024),)),
        "primal": draw_primal(jax.random.fold_in(key_list[7], 71), 0),
        "coarse_inverse": draw_coarse_inverse(jax.random.fold_in(key_list[7], 71), 0),
    }


spectrum_low = 1.0
spectrum_high = 16.0


def reorder(blocks):
    shaped = blocks.reshape(N_SUB, N_GRP, R, N_SUB, SLOT)
    return jnp.transpose(shaped, (3, 1, 2, 0, 4)).reshape(SUBS, R, M)


def visit_all(values, visit_rows):
    owners = values.reshape(R, SUBS, LAM)
    picked = jax.vmap(lambda block, indices: jnp.take(block, indices, axis=1), in_axes=(1, 0))(owners, visit_rows)
    return reorder(picked.astype(jnp.bfloat16))


def return_all(worked, visit_rows):
    moved = reorder(worked)
    summed = jax.vmap(lambda block, indices: jax.ops.segment_sum(block.astype(jnp.float32).T, indices, LAM))(moved, visit_rows)
    return jnp.transpose(summed, (2, 0, 1)).reshape(R, NLAM)


def dual_apply(values, visit_rows, dual_ops, coarse_maps, primal, coarse_inverse):
    visited = visit_all(values, visit_rows)

    def coarse_term(operands):
        return jnp.dot(operands[0], operands[1].T, preferred_element_type=jnp.float32).astype(jnp.bfloat16)

    contrib = lax.map(coarse_term, (visited, coarse_maps))
    flattened = jnp.transpose(contrib, (1, 0, 2)).reshape(R, SUBS * NP).astype(jnp.float32)
    assembled = jnp.zeros((R, NC), jnp.float32).at[:, primal.reshape(-1)].add(flattened)
    coarse = jnp.dot(assembled, coarse_inverse.astype(jnp.float32).T, precision=lax.Precision.HIGHEST).astype(jnp.bfloat16)
    corner_vals = jnp.transpose(jnp.take(coarse, primal, axis=1), (1, 0, 2))

    def local_step(items):
        seen_rows, matrix, coupling, corner_rows = items
        combined = seen_rows.astype(jnp.float32) + jnp.dot(seen_rows, matrix, preferred_element_type=jnp.float32)
        combined = combined + jnp.dot(corner_rows, coupling, preferred_element_type=jnp.float32)
        return combined.astype(jnp.bfloat16)

    worked = lax.map(local_step, (visited, dual_ops, coarse_maps, corner_vals))
    return return_all(worked, visit_rows)


def precondition(values, visit_rows, dirichlet_ops):
    visited = visit_all(values, visit_rows)

    def local_step(items):
        seen_rows, matrix = items
        combined = seen_rows.astype(jnp.float32) + jnp.dot(seen_rows, matrix, preferred_element_type=jnp.float32)
        return combined.astype(jnp.bfloat16)

    worked = lax.map(local_step, (visited, dirichlet_ops))
    return return_all(worked, visit_rows)


def reference(load, visit_rows, dual_ops, dirichlet_ops, coarse_maps, primal, coarse_inverse):
    center = 0.5 * (spectrum_high + spectrum_low)
    half_width = 0.5 * (spectrum_high - spectrum_low)
    stretch = center / half_width
    weight_now = 1.0 / stretch
    multipliers = jnp.zeros_like(load)
    residual = load
    direction = precondition(residual, visit_rows, dirichlet_ops) / center
    for iteration in range(ITERS):
        multipliers = multipliers + direction
        residual = residual - dual_apply(direction, visit_rows, dual_ops, coarse_maps, primal, coarse_inverse)
        if iteration + 1 < ITERS:
            smoothed = precondition(residual, visit_rows, dirichlet_ops)
            weight_next = 1.0 / (2.0 * stretch - weight_now)
            direction = (weight_next * weight_now) * direction + (2.0 * weight_next / half_width) * smoothed
            weight_now = weight_next
    return multipliers, residual
```

```python
import jax
import jax.numpy as jnp
from jax import lax
from jax.sharding import PartitionSpec as P

ITERS = 2
LANES = 128
LOW = 128

spectrum_low = 1.0
spectrum_high = 16.0


def body(load, visit_rows, dual_ops, dirichlet_ops, coarse_maps, primal, coarse_inverse):
    bf16, f32 = jnp.bfloat16, jnp.float32
    slot_rows = visit_rows[0]
    cases, owned = load.shape
    slots = slot_rows.shape[0]
    dual_block = dual_ops[0]
    dirichlet_block = dirichlet_ops[0]
    coupling = coarse_maps[0]
    corners = coupling.shape[0]
    band, total_coarse = coarse_inverse.shape
    groups = total_coarse // band
    subs = lax.axis_size("sub")
    share = slots // subs
    half = share // 2
    chunk = cases // subs
    group_corners = subs * corners
    high_count = total_coarse // LOW

    tally = (slot_rows[:, None] == jnp.arange(owned, dtype=jnp.int32)[None, :]).astype(bf16)

    def dot(left, right, contract):
        return lax.dot_general(left, right, (contract, ((), ())), preferred_element_type=f32)

    def swap_sub(blocks):
        return lax.all_to_all(blocks, "sub", split_axis=0, concat_axis=0, tiled=True)

    def swap_grp(blocks):
        return lax.all_to_all(blocks, "grp", split_axis=0, concat_axis=0, tiled=True)

    def pack(rows):
        blocks = rows.reshape(subs, 2, half, rows.shape[-1])
        return jnp.concatenate([blocks[:, 0], blocks[:, 1]], axis=-1)

    def unpack(blocks):
        width = blocks.shape[-1] // 2
        return jnp.stack([blocks[:, :, :width], blocks[:, :, width:]], axis=1).reshape(slots, width)

    def pick(values_low):
        return dot(tally, values_low, ((1,), (1,))).astype(bf16)

    def collect(blocks):
        return dot(unpack(blocks), tally, ((0,), (0,)))

    def local_apply(visited, matrix):
        return visited.astype(f32) + dot(matrix, visited, ((0,), (0,)))

    center = 0.5 * (spectrum_high + spectrum_low)
    half_width = 0.5 * (spectrum_high - spectrum_low)
    stretch = center / half_width
    weight_now = 1.0 / stretch

    own_coupling = pack(coupling.T)
    index_pair = jnp.stack([primal[0] // LOW, primal[0] % LOW], axis=-1).astype(bf16)
    extra = jnp.concatenate(
        [
            own_coupling,
            jnp.broadcast_to(index_pair[None], (subs, corners, 2)),
            jnp.zeros((subs, half, LANES - 2 * corners - 2), bf16),
        ],
        axis=-1,
    )
    first = swap_sub(jnp.concatenate([pack(pick(load.astype(bf16))), extra], axis=1))
    visited = unpack(first[:, :half])
    setup = first[:, half:]
    group_coupling = jnp.stack(
        [setup[:, :, :corners], setup[:, :, corners : 2 * corners]], axis=1
    ).reshape(subs, share, corners)
    owner_map = (
        lax.dot_general(
            group_coupling,
            tally.reshape(subs, share, owned),
            (((1,), (1,)), ((0,), (0,))),
            preferred_element_type=f32,
        )
        .astype(bf16)
        .reshape(group_corners, owned)
    )
    pair_rows = setup[:, :, 2 * corners : 2 * corners + 2].reshape(group_corners, 2).astype(jnp.int32)
    coarse_row = pair_rows[:, 0] * LOW + pair_rows[:, 1]

    def one_hot(which, count):
        return (which[:, None] == jnp.arange(count, dtype=jnp.int32)[None, :]).astype(bf16)

    high_mask = one_hot(pair_rows[:, 0], high_count)
    low_mask = one_hot(pair_rows[:, 1], LOW)
    group_mask = one_hot(coarse_row // band, groups)
    band_mask = one_hot(coarse_row % band, LANES)

    direction = collect(swap_sub(pack(local_apply(visited, dirichlet_block).astype(bf16)))) / center
    multipliers = jnp.zeros_like(load)
    residual = load
    for iteration in range(ITERS):
        multipliers = multipliers + direction
        direction_low = direction.astype(bf16)
        partial = dot(direction_low, owner_map, ((1,), (1,))).astype(bf16)
        arrived = swap_sub(
            jnp.concatenate(
                [pack(pick(direction_low)), partial.reshape(subs, -1, LANES)], axis=1
            )
        )
        visited = unpack(arrived[:, :half])
        contrib = (
            arrived[:, half:].astype(f32).sum(axis=0).reshape(chunk, group_corners).astype(bf16)
        )
        spread = contrib.T[:, :, None] * low_mask[:, None, :]
        piece = lax.dot_general(
            high_mask, spread, (((0,), (0,)), ((), ())), preferred_element_type=f32
        )
        piece = jnp.transpose(piece, (1, 0, 2)).reshape(groups, -1, LANES)
        slice_sum = swap_grp(piece).sum(axis=0)
        assembled = swap_grp(jnp.broadcast_to(slice_sum[None], (groups,) + slice_sum.shape))
        assembled = assembled.reshape(chunk, total_coarse)
        assembled_high = assembled.astype(bf16)
        assembled_low = (assembled - assembled_high.astype(f32)).astype(bf16)
        coarse_band = dot(
            jnp.concatenate([assembled_high, assembled_low]), coarse_inverse, ((1,), (1,))
        )
        coarse_band = (coarse_band[:chunk] + coarse_band[chunk:]).astype(bf16)
        coarse_band = jnp.pad(coarse_band, ((0, 0), (0, LANES - band)))
        coarse_all = swap_grp(jnp.broadcast_to(coarse_band[None], (groups, chunk, LANES)))
        candidate = lax.dot_general(
            group_mask, coarse_all, (((1,), (0,)), ((), ())), preferred_element_type=f32
        )
        corner_rows = (candidate * band_mask[:, None, :].astype(f32)).sum(axis=-1)
        corner_rows = corner_rows.T.astype(bf16).reshape(1, -1, LANES)
        worked = pack(local_apply(visited, dual_block).astype(bf16))
        arrived = swap_sub(
            jnp.concatenate(
                [worked, jnp.broadcast_to(corner_rows, (subs,) + corner_rows.shape[1:])], axis=1
            )
        )
        corner_all = arrived[:, half:].reshape(cases, group_corners)
        residual = residual - (
            collect(arrived[:, :half]) + dot(corner_all, owner_map, ((1,), (0,)))
        )
        if iteration + 1 < ITERS:
            visited = unpack(swap_sub(pack(pick(residual.astype(bf16)))))
            smoothed = collect(
                swap_sub(pack(local_apply(visited, dirichlet_block).astype(bf16)))
            )
            weight_next = 1.0 / (2.0 * stretch - weight_now)
            direction = (
                weight_next * weight_now * direction + 2.0 * weight_next / half_width * smoothed
            )
            weight_now = weight_next
    return (multipliers, residual)


def solution(mesh):
    placed = (
        P(None, ("sub", "grp")),
        P(("sub", "grp"), None),
        P(("sub", "grp"), None, None),
        P(("sub", "grp"), None, None),
        P(("sub", "grp"), None, None),
        P(("sub", "grp"), None),
        P("grp", None),
    )
    return jax.shard_map(
        body,
        mesh=mesh,
        in_specs=placed,
        out_specs=(P(None, ("sub", "grp")), P(None, ("sub", "grp"))),
        check_vma=False,
    )
```

```python
import functools

import jax
import jax.numpy as jnp
from jax import lax
from jax.experimental import pallas as pl
from jax.experimental.pallas import tpu as pltpu
from jax.sharding import PartitionSpec as P

ITERS = 2
LANES = 128
TAIL = 16
INTERPRET = False

spectrum_low = 1.0
spectrum_high = 16.0

bf16, f32 = jnp.bfloat16, jnp.float32


def call(kernel, outs, *args, flops=0):
    return pl.pallas_call(
        kernel,
        out_shape=tuple(jax.ShapeDtypeStruct(shape, kind) for shape, kind in outs),
        interpret=INTERPRET,
        compiler_params=pltpu.CompilerParams(vmem_limit_bytes=48 * 1024 * 1024),
        cost_estimate=pl.CostEstimate(flops=flops, bytes_accessed=1 << 20, transcendentals=0),
    )(*args)


def dot_nn(left, right):
    return lax.dot_general(left, right, (((1,), (0,)), ((), ())), preferred_element_type=f32)


def dot_nt(left, right):
    return lax.dot_general(left, right, (((1,), (1,)), ((), ())), preferred_element_type=f32)


def unpack(ref, half):
    rows = []
    for peer in range(ref.shape[0]):
        block = ref[peer, 0:half, :].astype(f32)
        width = block.shape[1] // 2
        rows += [block[:, :width], block[:, width:]]
    return jnp.concatenate(rows, axis=0)


def pack(rows, ref, half):
    for peer in range(ref.shape[0]):
        top = rows[2 * half * peer : 2 * half * peer + half]
        low = rows[2 * half * peer + half : 2 * half * (peer + 1)]
        ref[peer, 0:half, :] = jnp.concatenate([top, low], axis=1).astype(bf16)


def to_tail(rows):
    chunk, width = rows.shape
    parts = [rows[:, at : at + LANES] for at in range(0, width, LANES)]
    spare = TAIL - chunk * len(parts)
    return jnp.concatenate(parts + [jnp.zeros((spare, LANES), f32)], axis=0)


def from_tail(block, chunk, width):
    parts = [block[at * chunk : (at + 1) * chunk] for at in range(width // LANES)]
    return jnp.concatenate(parts, axis=1)


def local_kernel(recv, matrix_t, out, *, half):
    visited = unpack(recv, half)
    worked = visited + dot_nn(matrix_t[...], visited.astype(bf16))
    pack(worked, out, half)


def collect(recv, tally_t, half):
    return dot_nn(tally_t[...], unpack(recv, half).astype(bf16)).T


def direction_kernel(
    recv, tally, tally_t, owner_map, old, total, direction, multipliers, out, *, half, keep, gain
):
    smoothed = collect(recv, tally_t, half)
    if keep is None:
        fresh = smoothed / gain
        multipliers[...] = fresh
    else:
        fresh = keep * old[...] + gain * smoothed
        multipliers[...] = total[...] + fresh
    direction[...] = fresh
    low = fresh.astype(bf16)
    pack(dot_nt(tally[...], low), out, half)
    partial = dot_nt(low, owner_map[...])
    subs = out.shape[0]
    chunk = partial.shape[0] // subs
    for peer in range(subs):
        rows = partial[chunk * peer : chunk * (peer + 1)]
        out[peer, half : half + TAIL, :] = to_tail(rows).astype(bf16)


def contrib_kernel(recv, index_rows, out, *, half, chunk):
    width = index_rows.shape[1]
    total = recv[0, half : half + TAIL, :].astype(f32)
    for peer in range(1, recv.shape[0]):
        total = total + recv[peer, half : half + TAIL, :].astype(f32)
    rows = from_tail(total, chunk, width)
    block = jnp.concatenate([rows, index_rows[0 : 8 - chunk, :]], axis=0).astype(bf16)
    for group in range(out.shape[0]):
        out[group] = block


def coarse_kernel(recv, inverse, out, scratch, *, chunk):
    groups, rows, width = recv.shape
    band, total = inverse.shape
    high = total // LANES
    per = rows // chunk
    row_of = lax.broadcasted_iota(jnp.int32, (rows, width), 0) // chunk
    row_of = row_of.astype(f32)
    lane_of = lax.broadcasted_iota(jnp.int32, (LANES, width), 0).astype(f32)

    def step(group, so_far):
        block = recv[group].astype(f32)
        values = jnp.concatenate([block[0:chunk]] * per, axis=0)
        high_row = block[chunk : chunk + 1]
        low_row = block[chunk + 1 : chunk + 2]
        offset = high_row - row_of
        parts = [
            jnp.where(offset == float(per * at), values, 0.0) for at in range(high // per)
        ]
        spread = jnp.concatenate(parts, axis=0).astype(bf16)
        mask = jnp.where(lane_of == low_row, 1.0, 0.0).astype(bf16)
        return so_far + dot_nt(spread, mask)

    assembled = lax.fori_loop(0, groups, step, jnp.zeros((high * chunk, LANES), f32))
    flat = jnp.concatenate(
        [assembled[chunk * at : chunk * (at + 1)] for at in range(high)], axis=1
    )
    top = flat.astype(bf16).astype(f32)
    both = jnp.concatenate([top, flat - top], axis=0).astype(bf16)
    result = dot_nt(both, inverse[...])
    scratch[...] = jnp.zeros(scratch.shape, f32)
    scratch[0:chunk, 0:band] = result[0:chunk] + result[chunk : 2 * chunk]
    block = scratch[...].astype(bf16)
    for group in range(groups):
        out[group] = block


def corner_kernel(recv, index_rows, worked, out, *, half, chunk):
    width = index_rows.shape[1]
    groups = recv.shape[0] // 8
    group_row = index_rows[2:3, :]
    band_row = index_rows[3:4, :]
    lane_of = lax.broadcasted_iota(jnp.int32, (LANES, width), 0).astype(f32)
    mask = jnp.where(lane_of == band_row, 1.0, 0.0).astype(bf16)
    candidate = dot_nn(recv[...], mask)
    rows = jnp.zeros((8, width), f32)
    for group in range(groups):
        rows = rows + jnp.where(
            group_row == float(group), candidate[8 * group : 8 * group + 8], 0.0
        )
    block = to_tail(rows[0:chunk]).astype(bf16)
    for peer in range(out.shape[0]):
        out[peer, 0:half, :] = worked[peer]
        out[peer, half : half + TAIL, :] = block


def take_residual(recv, tally_t, owner_map, old, half):
    subs = recv.shape[0]
    cases = old.shape[0]
    corners = jnp.concatenate(
        [
            from_tail(
                recv[peer, half : half + TAIL, :].astype(f32), cases // subs, owner_map.shape[0]
            )
            for peer in range(subs)
        ],
        axis=0,
    )
    change = collect(recv, tally_t, half) + dot_nn(corners.astype(bf16), owner_map[...])
    return old[...] - change


def residual_kernel(recv, tally, tally_t, owner_map, old, residual, out, *, half):
    fresh = take_residual(recv, tally_t, owner_map, old, half)
    residual[...] = fresh
    pack(dot_nt(tally[...], fresh.astype(bf16)), out, half)


def last_kernel(recv, tally_t, owner_map, old, residual, *, half):
    residual[...] = take_residual(recv, tally_t, owner_map, old, half)


def body(load, visit_rows, dual_ops, dirichlet_ops, coarse_maps, primal, coarse_inverse):
    slot_rows = visit_rows[0]
    cases, owned = load.shape
    slots = slot_rows.shape[0]
    coupling = coarse_maps[0]
    corners = coupling.shape[0]
    band, total_coarse = coarse_inverse.shape
    groups = total_coarse // band
    subs = lax.axis_size("sub")
    share = slots // subs
    half = share // 2
    chunk = cases // subs
    group_corners = subs * corners

    tally = (slot_rows[:, None] == jnp.arange(owned, dtype=jnp.int32)[None, :]).astype(bf16)
    tally_t = (jnp.arange(owned, dtype=jnp.int32)[:, None] == slot_rows[None, :]).astype(bf16)

    def swap_sub(blocks):
        return lax.all_to_all(blocks, "sub", split_axis=0, concat_axis=0, tiled=True)

    def swap_grp(blocks):
        return lax.all_to_all(blocks, "grp", split_axis=0, concat_axis=0, tiled=True)

    def pack_plain(rows):
        blocks = rows.reshape(subs, 2, half, rows.shape[-1])
        return jnp.concatenate([blocks[:, 0], blocks[:, 1]], axis=-1)

    index_pair = jnp.stack([primal[0] // LANES, primal[0] % LANES], axis=-1).astype(bf16)
    extra = jnp.concatenate(
        [
            pack_plain(coupling.T),
            jnp.broadcast_to(index_pair[None], (subs, corners, 2)),
            jnp.zeros((subs, half, LANES - 2 * corners - 2), bf16),
        ],
        axis=-1,
    )
    picked = dot_nt(tally, load.astype(bf16)).astype(bf16)
    first = swap_sub(jnp.concatenate([pack_plain(picked), extra], axis=1))
    setup = first[:, half:]
    group_coupling = jnp.stack(
        [setup[:, :, :corners], setup[:, :, corners : 2 * corners]], axis=1
    ).reshape(subs, share, corners)
    owner_map = (
        lax.dot_general(
            group_coupling,
            tally.reshape(subs, share, owned),
            (((1,), (1,)), ((0,), (0,))),
            preferred_element_type=f32,
        )
        .astype(bf16)
        .reshape(group_corners, owned)
    )
    pair_rows = setup[:, :, 2 * corners : 2 * corners + 2].reshape(group_corners, 2)
    pair_rows = pair_rows.astype(f32).T
    coarse_row = pair_rows[0] * LANES + pair_rows[1]
    group_of = jnp.floor((coarse_row + 0.5) / band)
    zero = jnp.zeros_like(coarse_row)
    index_rows = jnp.stack(
        [pair_rows[0], pair_rows[1], group_of, coarse_row - group_of * band] + [zero] * 4
    )

    center = 0.5 * (spectrum_high + spectrum_low)
    half_width = 0.5 * (spectrum_high - spectrum_low)
    stretch = center / half_width
    weight_now = 1.0 / stretch

    dirichlet_t = dirichlet_ops[0].T
    dual_t = dual_ops[0].T
    square = 2 * slots * slots * cases
    packed = ((subs, half, 2 * cases), bf16)
    longer = ((subs, half + TAIL, 2 * cases), bf16)
    field = ((cases, owned), f32)

    def apply_local(arrived, matrix_t):
        kernel = functools.partial(local_kernel, half=half)
        return call(kernel, [packed], arrived, matrix_t, flops=square)[0]

    message = apply_local(first, dirichlet_t)
    keep, gain = None, center
    direction = multipliers = residual = load
    for iteration in range(ITERS):
        arrived = swap_sub(message)
        direction, multipliers, message = call(
            functools.partial(direction_kernel, half=half, keep=keep, gain=gain),
            [field, field, longer],
            arrived,
            tally,
            tally_t,
            owner_map,
            direction,
            multipliers,
            flops=square,
        )
        arrived = swap_sub(message)
        (message,) = call(
            functools.partial(contrib_kernel, half=half, chunk=chunk),
            [((groups, 8, group_corners), bf16)],
            arrived,
            index_rows,
        )
        contribs = swap_grp(message)
        worked = apply_local(arrived, dual_t)
        (message,) = pl.pallas_call(
            functools.partial(coarse_kernel, chunk=chunk),
            out_shape=(jax.ShapeDtypeStruct((groups, 8, LANES), bf16),),
            scratch_shapes=[pltpu.VMEM((8, LANES), f32)],
            interpret=INTERPRET,
            compiler_params=pltpu.CompilerParams(vmem_limit_bytes=48 * 1024 * 1024),
        )(contribs, coarse_inverse)
        coarse_all = swap_grp(message).reshape(8 * groups, LANES)
        (message,) = call(
            functools.partial(corner_kernel, half=half, chunk=chunk),
            [longer],
            coarse_all,
            index_rows,
            worked,
        )
        arrived = swap_sub(message)
        if iteration + 1 < ITERS:
            residual, message = call(
                functools.partial(residual_kernel, half=half),
                [field, packed],
                arrived,
                tally,
                tally_t,
                owner_map,
                residual,
                flops=square,
            )
            message = apply_local(swap_sub(message), dirichlet_t)
            weight_next = 1.0 / (2.0 * stretch - weight_now)
            keep = weight_next * weight_now
            gain = 2.0 * weight_next / half_width
            weight_now = weight_next
        else:
            (residual,) = call(
                functools.partial(last_kernel, half=half),
                [field],
                arrived,
                tally_t,
                owner_map,
                residual,
                flops=square,
            )
    return (multipliers, residual)


def solution(mesh):
    placed = (
        P(None, ("sub", "grp")),
        P(("sub", "grp"), None),
        P(("sub", "grp"), None, None),
        P(("sub", "grp"), None, None),
        P(("sub", "grp"), None, None),
        P(("sub", "grp"), None),
        P("grp", None),
    )
    return jax.shard_map(
        body,
        mesh=mesh,
        in_specs=placed,
        out_specs=(P(None, ("sub", "grp")), P(None, ("sub", "grp"))),
        check_vma=False,
    )
```

```python
import functools

import jax
import jax.numpy as jnp
from jax import lax
from jax.experimental import pallas as pl
from jax.experimental.pallas import tpu as pltpu
from jax.sharding import PartitionSpec as P

ITERS = 2
LANES = 128
TAIL = 16
INTERPRET = False

spectrum_low = 1.0
spectrum_high = 16.0

bf16, f32 = jnp.bfloat16, jnp.float32


def call(kernel, outs, *args, flops=0):
    return pl.pallas_call(
        kernel,
        out_shape=tuple(jax.ShapeDtypeStruct(shape, kind) for shape, kind in outs),
        interpret=INTERPRET,
        compiler_params=pltpu.CompilerParams(vmem_limit_bytes=48 * 1024 * 1024),
        cost_estimate=pl.CostEstimate(flops=flops, bytes_accessed=1 << 20, transcendentals=0),
    )(*args)


def far(array):
    if INTERPRET:
        return array
    return pltpu.with_memory_space_constraint(array, pltpu.HBM)


def dot_nn(left, right):
    return lax.dot_general(left, right, (((1,), (0,)), ((), ())), preferred_element_type=f32)


def dot_nt(left, right):
    return lax.dot_general(left, right, (((1,), (1,)), ((), ())), preferred_element_type=f32)


def unpack(ref, half):
    rows = []
    for peer in range(ref.shape[0]):
        block = ref[peer, 0:half, :].astype(f32)
        width = block.shape[1] // 2
        rows += [block[:, :width], block[:, width:]]
    return jnp.concatenate(rows, axis=0)


def pack(rows, ref, half):
    for peer in range(ref.shape[0]):
        top = rows[2 * half * peer : 2 * half * peer + half]
        low = rows[2 * half * peer + half : 2 * half * (peer + 1)]
        ref[peer, 0:half, :] = jnp.concatenate([top, low], axis=1).astype(bf16)


def to_tail(rows):
    chunk, width = rows.shape
    parts = [rows[:, at : at + LANES] for at in range(0, width, LANES)]
    spare = TAIL - chunk * len(parts)
    return jnp.concatenate(parts + [jnp.zeros((spare, LANES), f32)], axis=0)


def from_tail(block, chunk, width):
    parts = [block[at * chunk : (at + 1) * chunk] for at in range(width // LANES)]
    return jnp.concatenate(parts, axis=1)


def first_kernel(*refs, half):
    given, (out, scratch), held, ready = refs[:4], refs[4:6], refs[6:10], refs[10]
    copies = [pltpu.make_async_copy(given[at], held[at], ready.at[at]) for at in range(4)]
    for copy in copies:
        copy.start()
    for copy in copies:
        copy.wait()
    load, slot_rows, coupling, primal = held
    slots = slot_rows.shape[1]
    corners = coupling.shape[0]
    tally_t = tally_of(slot_rows, load.shape[1])
    pack(pick(load[...].astype(bf16), tally_t), out, half)
    spare = jnp.zeros((LANES - corners, slots), f32)
    columns = jnp.concatenate([coupling[...].astype(f32), spare], axis=0).T
    row = primal[...].astype(f32)
    high_row = jnp.floor((row + 0.5) / LANES)
    scratch[...] = jnp.zeros(scratch.shape, f32)
    scratch[0:1, LANES // 2 : LANES // 2 + corners] = high_row
    scratch[1:2, LANES // 2 : LANES // 2 + corners] = row - high_row * LANES
    for peer in range(out.shape[0]):
        top = 2 * half * peer
        scratch[:, 0:corners] = columns[top : top + half, 0:corners]
        scratch[:, corners : 2 * corners] = columns[top + half : top + 2 * half, 0:corners]
        out[peer, half : 2 * half, :] = scratch[...].astype(bf16)


def tally_of(slot_rows, owned):
    row_of = lax.broadcasted_iota(jnp.int32, (owned, slot_rows.shape[1]), 0)
    return jnp.where(row_of == slot_rows[...], 1.0, 0.0).astype(bf16)


def local_kernel(recv, matrix_t, out, *, half):
    visited = unpack(recv, half)
    worked = visited + dot_nn(matrix_t[...], visited.astype(bf16))
    pack(worked, out, half)


def collect(recv, tally_t, half):
    return dot_nn(tally_t, unpack(recv, half).astype(bf16)).T


def pick(values_low, tally_t):
    return dot_nn(values_low, tally_t).T


def direction_kernel(
    recv, slot_rows, owner_map, old, total, direction, multipliers, out, *, half, keep, gain
):
    tally_t = tally_of(slot_rows, direction.shape[1])
    smoothed = collect(recv, tally_t, half)
    if keep is None:
        fresh = smoothed / gain
        multipliers[...] = fresh
    else:
        fresh = keep * old[...] + gain * smoothed
        multipliers[...] = total[...] + fresh
    direction[...] = fresh
    low = fresh.astype(bf16)
    pack(pick(low, tally_t), out, half)
    partial = dot_nt(low, owner_map[...])
    subs = out.shape[0]
    chunk = partial.shape[0] // subs
    for peer in range(subs):
        rows = partial[chunk * peer : chunk * (peer + 1)]
        out[peer, half : half + TAIL, :] = to_tail(rows).astype(bf16)


def contrib_kernel(recv, *refs, half, chunk):
    out = refs[-1]
    total = recv[0, half : half + TAIL, :].astype(f32)
    for peer in range(1, recv.shape[0]):
        total = total + recv[peer, half : half + TAIL, :].astype(f32)
    rows = from_tail(total, chunk, out.shape[2])
    if len(refs) > 1:
        rows = jnp.concatenate([rows, refs[0][0 : out.shape[1] - chunk, :]], axis=0)
    block = rows.astype(bf16)
    for group in range(out.shape[0]):
        out[group] = block


def coarse_kernel(recv, places, inverse_far, out, scratch, inverse, ready, *, chunk, batch):
    copy = pltpu.make_async_copy(inverse_far, inverse, ready)
    copy.start()
    groups, _, width = recv.shape
    band, total = inverse.shape
    high = total // LANES
    per = TAIL // chunk
    row_of = (lax.broadcasted_iota(jnp.int32, (TAIL, width), 0) // chunk).astype(f32)
    lane_of = lax.broadcasted_iota(jnp.int32, (LANES, width), 0).astype(bf16)
    zero, one = jnp.zeros((), bf16), jnp.ones((), bf16)

    def factors(group):
        values = jnp.concatenate([recv[group].astype(f32)[0:chunk]] * per, axis=0).astype(bf16)
        place = places[group].astype(f32)[chunk : chunk + 2]
        offset = (place[0:1] - row_of).astype(bf16)
        parts = []
        for at in range(pl.cdiv(high, per)):
            part = jnp.where(offset == jnp.asarray(per * at, bf16), values, zero)
            parts.append(part)
        low_row = jnp.broadcast_to(place[1:2], (TAIL, width)).astype(bf16)
        low_row = jnp.concatenate([low_row] * (LANES // TAIL), axis=0)
        return jnp.concatenate(parts, axis=0), jnp.where(lane_of == low_row, one, zero)

    def step(at, so_far):
        both = [factors(at * batch + group) for group in range(batch)]
        spread = jnp.concatenate([pair[0] for pair in both], axis=1)
        mask = jnp.concatenate([pair[1] for pair in both], axis=1)
        return so_far + dot_nt(spread, mask)

    start = jnp.zeros((pl.cdiv(high, per) * TAIL, LANES), f32)
    assembled = lax.fori_loop(0, groups // batch, step, start)
    flat = jnp.concatenate(
        [assembled[chunk * at : chunk * (at + 1)] for at in range(high)], axis=1
    )
    top = flat.astype(bf16).astype(f32)
    both = jnp.concatenate([top, flat - top], axis=0).astype(bf16)
    copy.wait()
    result = dot_nt(both, inverse[...])
    scratch[...] = jnp.zeros(scratch.shape, f32)
    scratch[0:chunk, 0:band] = result[0:chunk] + result[chunk : 2 * chunk]
    block = scratch[...].astype(bf16)
    for group in range(groups):
        out[group] = block


def corner_kernel(recv, index_rows, worked, out, *, half, chunk):
    width = index_rows.shape[1]
    groups = recv.shape[0] // 8
    group_row = index_rows[2:3, :]
    band_row = index_rows[3:4, :]
    lane_of = lax.broadcasted_iota(jnp.int32, (LANES, width), 0).astype(f32)
    mask = jnp.where(lane_of == band_row, 1.0, 0.0).astype(bf16)
    candidate = dot_nn(recv[...], mask)
    rows = jnp.zeros((8, width), f32)
    for group in range(groups):
        rows = rows + jnp.where(
            group_row == float(group), candidate[8 * group : 8 * group + 8], 0.0
        )
    block = to_tail(rows[0:chunk]).astype(bf16)
    for peer in range(out.shape[0]):
        out[peer, 0:half, :] = worked[peer]
        out[peer, half : half + TAIL, :] = block


def take_residual(recv, tally_t, owner_map, old, half):
    subs = recv.shape[0]
    cases = old.shape[0]
    corners = jnp.concatenate(
        [
            from_tail(
                recv[peer, half : half + TAIL, :].astype(f32), cases // subs, owner_map.shape[0]
            )
            for peer in range(subs)
        ],
        axis=0,
    )
    change = collect(recv, tally_t, half) + dot_nn(corners.astype(bf16), owner_map[...])
    return old[...] - change


def residual_kernel(recv, slot_rows, owner_map, old, residual, out, *, half):
    tally_t = tally_of(slot_rows, old.shape[1])
    fresh = take_residual(recv, tally_t, owner_map, old, half)
    residual[...] = fresh
    pack(pick(fresh.astype(bf16), tally_t), out, half)


def last_kernel(recv, slot_rows, owner_map, old, residual, *, half):
    tally_t = tally_of(slot_rows, old.shape[1])
    residual[...] = take_residual(recv, tally_t, owner_map, old, half)


def body(load, visit_rows, dual_ops, dirichlet_ops, coarse_maps, primal, coarse_inverse):
    slot_rows = visit_rows[0]
    cases, owned = load.shape
    slots = slot_rows.shape[0]
    coupling = coarse_maps[0]
    corners = coupling.shape[0]
    band, total_coarse = coarse_inverse.shape
    groups = total_coarse // band
    subs = lax.axis_size("sub")
    share = slots // subs
    half = share // 2
    chunk = cases // subs
    group_corners = subs * corners

    tally = (slot_rows[:, None] == jnp.arange(owned, dtype=jnp.int32)[None, :]).astype(bf16)

    def swap_sub(blocks):
        return lax.all_to_all(blocks, "sub", split_axis=0, concat_axis=0, tiled=True)

    def swap_grp(blocks):
        return lax.all_to_all(blocks, "grp", split_axis=0, concat_axis=0, tiled=True)

    (message,) = pl.pallas_call(
        functools.partial(first_kernel, half=half),
        out_shape=(jax.ShapeDtypeStruct((subs, 2 * half, LANES), bf16),),
        in_specs=[pl.BlockSpec(memory_space=pltpu.HBM)] * 4,
        scratch_shapes=[pltpu.VMEM((half, LANES), f32)]
        + [pltpu.VMEM(x.shape, x.dtype) for x in (load, visit_rows, coupling, primal)]
        + [pltpu.SemaphoreType.DMA((4,))],
        interpret=INTERPRET,
        compiler_params=pltpu.CompilerParams(vmem_limit_bytes=48 * 1024 * 1024),
    )(*(far(x) for x in (load, visit_rows, coupling, primal)))
    first = swap_sub(message)
    setup = first[:, half:]
    group_coupling = jnp.stack(
        [setup[:, :, :corners], setup[:, :, corners : 2 * corners]], axis=1
    ).reshape(subs, share, corners)
    owner_map = (
        lax.dot_general(
            group_coupling,
            tally.reshape(subs, share, owned),
            (((1,), (1,)), ((0,), (0,))),
            preferred_element_type=f32,
        )
        .astype(bf16)
        .reshape(group_corners, owned)
    )
    pair_rows = setup[:, 0:2, LANES // 2 : LANES // 2 + corners]
    pair_rows = jnp.transpose(pair_rows, (1, 0, 2)).reshape(2, group_corners)
    pair_rows = pair_rows.astype(f32)
    coarse_row = pair_rows[0] * LANES + pair_rows[1]
    group_of = jnp.floor((coarse_row + 0.5) / band)
    zero = jnp.zeros_like(coarse_row)
    index_rows = jnp.stack(
        [pair_rows[0], pair_rows[1], group_of, coarse_row - group_of * band] + [zero] * 4
    )

    center = 0.5 * (spectrum_high + spectrum_low)
    half_width = 0.5 * (spectrum_high - spectrum_low)
    stretch = center / half_width
    weight_now = 1.0 / stretch

    dirichlet_t = dirichlet_ops[0].T
    dual_t = dual_ops[0].T
    square = 2 * slots * slots * cases
    packed = ((subs, half, 2 * cases), bf16)
    longer = ((subs, half + TAIL, 2 * cases), bf16)
    field = ((cases, owned), f32)

    def apply_local(arrived, matrix_t):
        kernel = functools.partial(local_kernel, half=half)
        return call(kernel, [packed], arrived, matrix_t, flops=square)[0]

    message = apply_local(first, dirichlet_t)
    keep, gain = None, center
    direction = multipliers = residual = load
    for iteration in range(ITERS):
        arrived = swap_sub(message)
        direction, multipliers, message = call(
            functools.partial(direction_kernel, half=half, keep=keep, gain=gain),
            [field, field, longer],
            arrived,
            visit_rows,
            owner_map,
            direction,
            multipliers,
            flops=square,
        )
        arrived = swap_sub(message)
        (message,) = call(
            functools.partial(contrib_kernel, half=half, chunk=chunk),
            [((groups, chunk if iteration else 8, group_corners), bf16)],
            *((arrived,) if iteration else (arrived, index_rows)),
        )
        contribs = swap_grp(message)
        places = places if iteration else contribs
        worked = apply_local(arrived, dual_t)
        (message,) = pl.pallas_call(
            functools.partial(coarse_kernel, chunk=chunk, batch=min(16, groups)),
            out_shape=(jax.ShapeDtypeStruct((groups, 8, LANES), bf16),),
            in_specs=[
                pl.BlockSpec(memory_space=pltpu.VMEM),
                pl.BlockSpec(memory_space=pltpu.VMEM),
                pl.BlockSpec(memory_space=pltpu.HBM),
            ],
            scratch_shapes=[
                pltpu.VMEM((8, LANES), f32),
                pltpu.VMEM(coarse_inverse.shape, bf16),
                pltpu.SemaphoreType.DMA,
            ],
            interpret=INTERPRET,
            compiler_params=pltpu.CompilerParams(vmem_limit_bytes=48 * 1024 * 1024),
        )(contribs, places, far(coarse_inverse))
        coarse_all = swap_grp(message).reshape(8 * groups, LANES)
        (message,) = call(
            functools.partial(corner_kernel, half=half, chunk=chunk),
            [longer],
            coarse_all,
            index_rows,
            worked,
        )
        arrived = swap_sub(message)
        if iteration + 1 < ITERS:
            residual, message = call(
                functools.partial(residual_kernel, half=half),
                [field, packed],
                arrived,
                visit_rows,
                owner_map,
                residual,
                flops=square,
            )
            message = apply_local(swap_sub(message), dirichlet_t)
            weight_next = 1.0 / (2.0 * stretch - weight_now)
            keep = weight_next * weight_now
            gain = 2.0 * weight_next / half_width
            weight_now = weight_next
        else:
            (residual,) = call(
                functools.partial(last_kernel, half=half),
                [field],
                arrived,
                visit_rows,
                owner_map,
                residual,
                flops=square,
            )
    return (multipliers, residual)


def solution(mesh):
    placed = (
        P(None, ("sub", "grp")),
        P(("sub", "grp"), None),
        P(("sub", "grp"), None, None),
        P(("sub", "grp"), None, None),
        P(("sub", "grp"), None, None),
        P(("sub", "grp"), None),
        P("grp", None),
    )
    return jax.shard_map(
        body,
        mesh=mesh,
        in_specs=placed,
        out_specs=(P(None, ("sub", "grp")), P(None, ("sub", "grp"))),
        check_vma=False,
    )
```

```python
import functools

import jax
import jax.numpy as jnp
from jax import lax
from jax.experimental import pallas as pl
from jax.experimental.pallas import tpu as pltpu
from jax.sharding import PartitionSpec as P

ITERS = 2
LANES = 128
TAIL = 16
INTERPRET = False

spectrum_low = 1.0
spectrum_high = 16.0

bf16, f32 = jnp.bfloat16, jnp.float32


def call(kernel, outs, *args, flops=0):
    return pl.pallas_call(
        kernel,
        out_shape=tuple(jax.ShapeDtypeStruct(shape, kind) for shape, kind in outs),
        interpret=INTERPRET,
        compiler_params=pltpu.CompilerParams(vmem_limit_bytes=48 * 1024 * 1024),
        cost_estimate=pl.CostEstimate(flops=flops, bytes_accessed=1 << 20, transcendentals=0),
    )(*args)


def far(array):
    if INTERPRET:
        return array
    return pltpu.with_memory_space_constraint(array, pltpu.HBM)


def dot_nn(left, right):
    return lax.dot_general(left, right, (((1,), (0,)), ((), ())), preferred_element_type=f32)


def dot_nt(left, right):
    return lax.dot_general(left, right, (((1,), (1,)), ((), ())), preferred_element_type=f32)


def unpack(ref, half):
    rows = []
    for peer in range(ref.shape[0]):
        block = ref[peer, 0:half, :].astype(f32)
        width = block.shape[1] // 2
        rows += [block[:, :width], block[:, width:]]
    return jnp.concatenate(rows, axis=0)


def pack(rows, ref, half):
    for peer in range(ref.shape[0]):
        top = rows[2 * half * peer : 2 * half * peer + half]
        low = rows[2 * half * peer + half : 2 * half * (peer + 1)]
        ref[peer, 0:half, :] = jnp.concatenate([top, low], axis=1).astype(bf16)


def to_tail(rows):
    chunk, width = rows.shape
    parts = [rows[:, at : at + LANES] for at in range(0, width, LANES)]
    spare = TAIL - chunk * len(parts)
    return jnp.concatenate(parts + [jnp.zeros((spare, LANES), f32)], axis=0)


def from_tail(block, chunk, width):
    parts = [block[at * chunk : (at + 1) * chunk] for at in range(width // LANES)]
    return jnp.concatenate(parts, axis=1)


def first_kernel(*refs, half):
    given, (out, scratch), held, ready = refs[:4], refs[4:6], refs[6:10], refs[10]
    copies = [pltpu.make_async_copy(given[at], held[at], ready.at[at]) for at in range(4)]
    for copy in copies:
        copy.start()
    for copy in copies:
        copy.wait()
    load, slot_rows, coupling, primal = held
    slots = slot_rows.shape[1]
    corners = coupling.shape[0]
    tally_t = tally_of(slot_rows, load.shape[1])
    pack(pick(load[...].astype(bf16), tally_t), out, half)
    spare = jnp.zeros((LANES - corners, slots), f32)
    columns = jnp.concatenate([coupling[...].astype(f32), spare], axis=0).T
    row = primal[...].astype(f32)
    high_row = jnp.floor((row + 0.5) / LANES)
    scratch[...] = jnp.zeros(scratch.shape, f32)
    scratch[0:1, LANES - 2 * TAIL : LANES - 2 * TAIL + corners] = high_row
    scratch[1:2, LANES - 2 * TAIL : LANES - 2 * TAIL + corners] = row - high_row * LANES
    for peer in range(out.shape[0]):
        for part in range(2 * half // TAIL):
            top = 2 * half * peer + TAIL * part
            scratch[:, corners * part : corners * (part + 1)] = columns[top : top + TAIL, 0:corners]
        out[peer, half : half + TAIL, :] = scratch[...].astype(bf16)


def tally_of(slot_rows, owned):
    row_of = lax.broadcasted_iota(jnp.int32, (owned, slot_rows.shape[1]), 0)
    return jnp.where(row_of == slot_rows[...], 1.0, 0.0).astype(bf16)


def local_kernel(recv, matrix_t, out, *, half):
    visited = unpack(recv, half)
    worked = visited + dot_nn(matrix_t[...], visited.astype(bf16))
    pack(worked, out, half)


def collect(recv, tally_t, half):
    return dot_nn(tally_t, unpack(recv, half).astype(bf16)).T


def pick(values_low, tally_t):
    return dot_nn(values_low, tally_t).T


def direction_kernel(
    recv, slot_rows, owner_map, old, total, direction, multipliers, out, *, half, keep, gain
):
    tally_t = tally_of(slot_rows, direction.shape[1])
    smoothed = collect(recv, tally_t, half)
    if keep is None:
        fresh = smoothed / gain
        multipliers[...] = fresh
    else:
        fresh = keep * old[...] + gain * smoothed
        multipliers[...] = total[...] + fresh
    direction[...] = fresh
    low = fresh.astype(bf16)
    pack(pick(low, tally_t), out, half)
    partial = dot_nt(low, owner_map[...])
    subs = out.shape[0]
    chunk = partial.shape[0] // subs
    for peer in range(subs):
        rows = partial[chunk * peer : chunk * (peer + 1)]
        out[peer, half : half + TAIL, :] = to_tail(rows).astype(bf16)


def contrib_kernel(recv, *refs, half, chunk, width):
    out = refs[-1]
    total = recv[0, half : half + TAIL, :].astype(f32)
    for peer in range(1, recv.shape[0]):
        total = total + recv[peer, half : half + TAIL, :].astype(f32)
    rows = from_tail(total, chunk, width)
    parts = [rows[0 : chunk // 2], rows[chunk // 2 : chunk]]
    if len(refs) > 1:
        parts.append(refs[0][0 : chunk // 2, :])
    rows = jnp.concatenate(parts, axis=1)
    block = rows.astype(bf16)
    for group in range(out.shape[0]):
        out[group] = block


def coarse_kernel(recv, places, inverse_far, out, scratch, inverse, ready, *, chunk, batch):
    copy = pltpu.make_async_copy(inverse_far, inverse, ready)
    copy.start()
    groups = recv.shape[0]
    width = places.shape[2] // 3
    band, total = inverse.shape
    high = total // LANES
    per = TAIL // chunk
    row_of = (lax.broadcasted_iota(jnp.int32, (TAIL, width), 0) // chunk).astype(f32)
    lane_of = lax.broadcasted_iota(jnp.int32, (LANES, width), 0).astype(bf16)
    zero, one = jnp.zeros((), bf16), jnp.ones((), bf16)

    def factors(group):
        pairs = recv[group].astype(f32)
        halves = [pairs[:, 0:width], pairs[:, width : 2 * width]]
        values = jnp.concatenate(halves * per, axis=0).astype(bf16)
        place = places[group].astype(f32)[:, 2 * width :]
        offset = (place[0:1] - row_of).astype(bf16)
        parts = []
        for at in range(pl.cdiv(high, per)):
            part = jnp.where(offset == jnp.asarray(per * at, bf16), values, zero)
            parts.append(part)
        low_row = jnp.broadcast_to(place[1:2], (TAIL, width)).astype(bf16)
        low_row = jnp.concatenate([low_row] * (LANES // TAIL), axis=0)
        return jnp.concatenate(parts, axis=0), jnp.where(lane_of == low_row, one, zero)

    def step(at, so_far):
        both = [factors(at * batch + group) for group in range(batch)]
        spread = jnp.concatenate([pair[0] for pair in both], axis=1)
        mask = jnp.concatenate([pair[1] for pair in both], axis=1)
        return so_far + dot_nt(spread, mask)

    start = jnp.zeros((pl.cdiv(high, per) * TAIL, LANES), f32)
    assembled = lax.fori_loop(0, groups // batch, step, start)
    flat = jnp.concatenate(
        [assembled[chunk * at : chunk * (at + 1)] for at in range(high)], axis=1
    )
    top = flat.astype(bf16).astype(f32)
    both = jnp.concatenate([top, flat - top], axis=0).astype(bf16)
    copy.wait()
    result = dot_nt(both, inverse[...])
    scratch[...] = jnp.zeros(scratch.shape, f32)
    scratch[:, 0:band] = result[0:chunk] + result[chunk : 2 * chunk]
    block = scratch[...].astype(bf16)
    for group in range(groups):
        out[group] = block


def corner_kernel(recv, index_rows, worked, out, *, half, chunk):
    width = index_rows.shape[1]
    groups = recv.shape[0]
    group_row = index_rows[2:3, :]
    band_row = index_rows[3:4, :]
    lane_of = lax.broadcasted_iota(jnp.int32, (LANES, width), 0).astype(f32)
    mask = jnp.where(lane_of == band_row, 1.0, 0.0).astype(bf16)
    coarse = jnp.concatenate([recv[group].astype(f32) for group in range(groups)], axis=0)
    candidate = dot_nn(coarse.astype(bf16), mask)
    which = group_row - (lax.broadcasted_iota(jnp.int32, (8, width), 0) // chunk).astype(f32)
    rows = jnp.zeros((8, width), f32)
    for at in range(0, groups * chunk, 8):
        rows = rows + jnp.where(which == float(at // chunk), candidate[at : at + 8], 0.0)
    rows = rows[0:chunk] + rows[chunk : 2 * chunk]
    block = to_tail(rows).astype(bf16)
    for peer in range(out.shape[0]):
        out[peer, 0:half, :] = worked[peer]
        out[peer, half : half + TAIL, :] = block


def take_residual(recv, tally_t, owner_map, old, half):
    subs = recv.shape[0]
    cases = old.shape[0]
    corners = jnp.concatenate(
        [
            from_tail(
                recv[peer, half : half + TAIL, :].astype(f32), cases // subs, owner_map.shape[0]
            )
            for peer in range(subs)
        ],
        axis=0,
    )
    change = collect(recv, tally_t, half) + dot_nn(corners.astype(bf16), owner_map[...])
    return old[...] - change


def residual_kernel(recv, slot_rows, owner_map, old, residual, out, *, half):
    tally_t = tally_of(slot_rows, old.shape[1])
    fresh = take_residual(recv, tally_t, owner_map, old, half)
    residual[...] = fresh
    pack(pick(fresh.astype(bf16), tally_t), out, half)


def last_kernel(recv, slot_rows, owner_map, old, residual, *, half):
    tally_t = tally_of(slot_rows, old.shape[1])
    residual[...] = take_residual(recv, tally_t, owner_map, old, half)


def body(load, visit_rows, dual_ops, dirichlet_ops, coarse_maps, primal, coarse_inverse):
    slot_rows = visit_rows[0]
    cases, owned = load.shape
    slots = slot_rows.shape[0]
    coupling = coarse_maps[0]
    corners = coupling.shape[0]
    band, total_coarse = coarse_inverse.shape
    groups = total_coarse // band
    subs = lax.axis_size("sub")
    share = slots // subs
    half = share // 2
    chunk = cases // subs
    group_corners = subs * corners

    tally = (slot_rows[:, None] == jnp.arange(owned, dtype=jnp.int32)[None, :]).astype(bf16)

    def swap_sub(blocks):
        return lax.all_to_all(blocks, "sub", split_axis=0, concat_axis=0, tiled=True)

    def swap_grp(blocks):
        return lax.all_to_all(blocks, "grp", split_axis=0, concat_axis=0, tiled=True)

    (message,) = pl.pallas_call(
        functools.partial(first_kernel, half=half),
        out_shape=(jax.ShapeDtypeStruct((subs, half + TAIL, LANES), bf16),),
        in_specs=[pl.BlockSpec(memory_space=pltpu.HBM)] * 4,
        scratch_shapes=[pltpu.VMEM((TAIL, LANES), f32)]
        + [pltpu.VMEM(x.shape, x.dtype) for x in (load, visit_rows, coupling, primal)]
        + [pltpu.SemaphoreType.DMA((4,))],
        interpret=INTERPRET,
        compiler_params=pltpu.CompilerParams(vmem_limit_bytes=48 * 1024 * 1024),
    )(*(far(x) for x in (load, visit_rows, coupling, primal)))
    first = swap_sub(message)
    setup = first[:, half:]
    group_coupling = jnp.stack(
        [setup[:, :, corners * at : corners * (at + 1)] for at in range(share // TAIL)], axis=1
    ).reshape(subs, share, corners)
    owner_map = (
        lax.dot_general(
            group_coupling,
            tally.reshape(subs, share, owned),
            (((1,), (1,)), ((0,), (0,))),
            preferred_element_type=f32,
        )
        .astype(bf16)
        .reshape(group_corners, owned)
    )
    pair_rows = setup[:, 0:2, LANES - 2 * TAIL : LANES - 2 * TAIL + corners]
    pair_rows = jnp.transpose(pair_rows, (1, 0, 2)).reshape(2, group_corners)
    pair_rows = pair_rows.astype(f32)
    coarse_row = pair_rows[0] * LANES + pair_rows[1]
    group_of = jnp.floor((coarse_row + 0.5) / band)
    zero = jnp.zeros_like(coarse_row)
    index_rows = jnp.stack(
        [pair_rows[0], pair_rows[1], group_of, coarse_row - group_of * band] + [zero] * 4
    )

    center = 0.5 * (spectrum_high + spectrum_low)
    half_width = 0.5 * (spectrum_high - spectrum_low)
    stretch = center / half_width
    weight_now = 1.0 / stretch

    dirichlet_t = dirichlet_ops[0].T
    dual_t = dual_ops[0].T
    square = 2 * slots * slots * cases
    packed = ((subs, half, 2 * cases), bf16)
    longer = ((subs, half + TAIL, 2 * cases), bf16)
    field = ((cases, owned), f32)

    def apply_local(arrived, matrix_t):
        kernel = functools.partial(local_kernel, half=half)
        return call(kernel, [packed], arrived, matrix_t, flops=square)[0]

    message = apply_local(first, dirichlet_t)
    keep, gain = None, center
    direction = multipliers = residual = load
    for iteration in range(ITERS):
        arrived = swap_sub(message)
        direction, multipliers, message = call(
            functools.partial(direction_kernel, half=half, keep=keep, gain=gain),
            [field, field, longer],
            arrived,
            visit_rows,
            owner_map,
            direction,
            multipliers,
            flops=square,
        )
        arrived = swap_sub(message)
        (message,) = call(
            functools.partial(contrib_kernel, half=half, chunk=chunk, width=group_corners),
            [((groups, chunk // 2, (2 if iteration else 3) * group_corners), bf16)],
            *((arrived,) if iteration else (arrived, index_rows)),
        )
        contribs = swap_grp(message)
        places = places if iteration else contribs
        worked = apply_local(arrived, dual_t)
        (message,) = pl.pallas_call(
            functools.partial(coarse_kernel, chunk=chunk, batch=min(32, groups)),
            out_shape=(jax.ShapeDtypeStruct((groups, chunk, LANES), bf16),),
            in_specs=[
                pl.BlockSpec(memory_space=pltpu.VMEM),
                pl.BlockSpec(memory_space=pltpu.VMEM),
                pl.BlockSpec(memory_space=pltpu.HBM),
            ],
            scratch_shapes=[
                pltpu.VMEM((chunk, LANES), f32),
                pltpu.VMEM(coarse_inverse.shape, bf16),
                pltpu.SemaphoreType.DMA,
            ],
            interpret=INTERPRET,
            compiler_params=pltpu.CompilerParams(vmem_limit_bytes=48 * 1024 * 1024),
        )(contribs, places, far(coarse_inverse))
        coarse_all = swap_grp(message)
        (message,) = call(
            functools.partial(corner_kernel, half=half, chunk=chunk),
            [longer],
            coarse_all,
            index_rows,
            worked,
        )
        arrived = swap_sub(message)
        if iteration + 1 < ITERS:
            residual, message = call(
                functools.partial(residual_kernel, half=half),
                [field, packed],
                arrived,
                visit_rows,
                owner_map,
                residual,
                flops=square,
            )
            message = apply_local(swap_sub(message), dirichlet_t)
            weight_next = 1.0 / (2.0 * stretch - weight_now)
            keep = weight_next * weight_now
            gain = 2.0 * weight_next / half_width
            weight_now = weight_next
        else:
            (residual,) = call(
                functools.partial(last_kernel, half=half),
                [field],
                arrived,
                visit_rows,
                owner_map,
                residual,
                flops=square,
            )
    return (multipliers, residual)


def solution(mesh):
    placed = (
        P(None, ("sub", "grp")),
        P(("sub", "grp"), None),
        P(("sub", "grp"), None, None),
        P(("sub", "grp"), None, None),
        P(("sub", "grp"), None, None),
        P(("sub", "grp"), None),
        P("grp", None),
    )
    return jax.shard_map(
        body,
        mesh=mesh,
        in_specs=placed,
        out_specs=(P(None, ("sub", "grp")), P(None, ("sub", "grp"))),
        check_vma=False,
    )
```

```python
import functools

import jax
import jax.numpy as jnp
from jax import lax
from jax.experimental import pallas as pl
from jax.experimental.pallas import tpu as pltpu
from jax.sharding import PartitionSpec as P

ITERS = 2
LANES = 128
TAIL = 16
INTERPRET = False

spectrum_low = 1.0
spectrum_high = 16.0

bf16, f32 = jnp.bfloat16, jnp.float32


def call(kernel, outs, *args, flops=0):
    return pl.pallas_call(
        kernel,
        out_shape=tuple(jax.ShapeDtypeStruct(shape, kind) for shape, kind in outs),
        interpret=INTERPRET,
        compiler_params=pltpu.CompilerParams(vmem_limit_bytes=48 * 1024 * 1024),
        cost_estimate=pl.CostEstimate(flops=flops, bytes_accessed=1 << 20, transcendentals=0),
    )(*args)


def far(array):
    if INTERPRET:
        return array
    return pltpu.with_memory_space_constraint(array, pltpu.HBM)


def dot_nn(left, right):
    return lax.dot_general(left, right, (((1,), (0,)), ((), ())), preferred_element_type=f32)


def dot_nt(left, right):
    return lax.dot_general(left, right, (((1,), (1,)), ((), ())), preferred_element_type=f32)


def unpack(ref, half):
    rows = []
    for peer in range(ref.shape[0]):
        block = ref[peer, 0:half, :].astype(f32)
        width = block.shape[1] // 2
        rows += [block[:, :width], block[:, width:]]
    return jnp.concatenate(rows, axis=0)


def pack(rows, ref, half):
    for peer in range(ref.shape[0]):
        top = rows[2 * half * peer : 2 * half * peer + half]
        low = rows[2 * half * peer + half : 2 * half * (peer + 1)]
        ref[peer, 0:half, :] = jnp.concatenate([top, low], axis=1).astype(bf16)


def to_tail(rows):
    chunk, width = rows.shape
    parts = [rows[:, at : at + LANES] for at in range(0, width, LANES)]
    spare = TAIL - chunk * len(parts)
    return jnp.concatenate(parts + [jnp.zeros((spare, LANES), f32)], axis=0)


def from_tail(block, chunk, width):
    parts = [block[at * chunk : (at + 1) * chunk] for at in range(width // LANES)]
    return jnp.concatenate(parts, axis=1)


def first_kernel(*refs, half):
    given, (out, scratch), held, ready = refs[:4], refs[4:6], refs[6:10], refs[10]
    copies = [pltpu.make_async_copy(given[at], held[at], ready.at[at]) for at in range(4)]
    for copy in copies:
        copy.start()
    for copy in copies:
        copy.wait()
    load, slot_rows, coupling, primal = held
    slots = slot_rows.shape[1]
    corners = coupling.shape[0]
    tally_t = tally_of(slot_rows, load.shape[1])
    pack(pick(load[...].astype(bf16), tally_t), out, half)
    spare = jnp.zeros((LANES - corners, slots), f32)
    columns = jnp.concatenate([coupling[...].astype(f32), spare], axis=0).T
    row = primal[...].astype(f32)
    high_row = jnp.floor((row + 0.5) / LANES)
    scratch[...] = jnp.zeros(scratch.shape, f32)
    scratch[0:1, LANES - 2 * TAIL : LANES - 2 * TAIL + corners] = high_row
    scratch[1:2, LANES - 2 * TAIL : LANES - 2 * TAIL + corners] = row - high_row * LANES
    for peer in range(out.shape[0]):
        for part in range(2 * half // TAIL):
            top = 2 * half * peer + TAIL * part
            scratch[:, corners * part : corners * (part + 1)] = columns[top : top + TAIL, 0:corners]
        out[peer, half : half + TAIL, :] = scratch[...].astype(bf16)


def tally_of(slot_rows, owned):
    row_of = lax.broadcasted_iota(jnp.int32, (owned, slot_rows.shape[1]), 0)
    return jnp.where(row_of == slot_rows[...], 1.0, 0.0).astype(bf16)


def local_kernel(recv, matrix_t, out, *, half):
    visited = unpack(recv, half)
    worked = visited + dot_nn(matrix_t[...], visited.astype(bf16))
    pack(worked, out, half)


def collect(recv, tally_t, half):
    return dot_nn(tally_t, unpack(recv, half).astype(bf16)).T


def pick(values_low, tally_t):
    return dot_nn(values_low, tally_t).T


def direction_kernel(
    recv, slot_rows, owner_map, old, field, out, *, half, keep, gain
):
    tally_t = tally_of(slot_rows, field.shape[1])
    smoothed = collect(recv, tally_t, half)
    if keep is None:
        fresh = smoothed / gain
        field[...] = fresh
    else:
        fresh = keep * old[...] + gain * smoothed
        field[...] = old[...] + fresh
    low = fresh.astype(bf16)
    pack(pick(low, tally_t), out, half)
    partial = dot_nt(low, owner_map[...])
    subs = out.shape[0]
    chunk = partial.shape[0] // subs
    for peer in range(subs):
        rows = partial[chunk * peer : chunk * (peer + 1)]
        out[peer, half : half + TAIL, :] = to_tail(rows).astype(bf16)


def contrib_kernel(recv, *refs, half, chunk, width):
    out = refs[-1]
    total = recv[0, half : half + TAIL, :].astype(f32)
    for peer in range(1, recv.shape[0]):
        total = total + recv[peer, half : half + TAIL, :].astype(f32)
    rows = from_tail(total, chunk, width)
    parts = [rows[0 : chunk // 2], rows[chunk // 2 : chunk]]
    if len(refs) > 1:
        parts.append(refs[0][0 : chunk // 2, :])
    rows = jnp.concatenate(parts, axis=1)
    block = rows.astype(bf16)
    for group in range(out.shape[0]):
        out[group] = block


def coarse_kernel(recv, places, inverse_far, out, scratch, inverse, ready, *, chunk, batch):
    copy = pltpu.make_async_copy(inverse_far, inverse, ready)
    copy.start()
    groups = recv.shape[0]
    width = places.shape[2] // 3
    band, total = inverse.shape
    high = total // LANES
    per = TAIL // chunk
    row_of = (lax.broadcasted_iota(jnp.int32, (TAIL, width), 0) // chunk).astype(f32)
    lane_of = lax.broadcasted_iota(jnp.int32, (LANES, width), 0).astype(bf16)
    zero, one = jnp.zeros((), bf16), jnp.ones((), bf16)

    def factors(group):
        pairs = recv[group].astype(f32)
        halves = [pairs[:, 0:width], pairs[:, width : 2 * width]]
        values = jnp.concatenate(halves * per, axis=0).astype(bf16)
        place = places[group].astype(f32)[:, 2 * width :]
        offset = (place[0:1] - row_of).astype(bf16)
        parts = []
        for at in range(pl.cdiv(high, per)):
            part = jnp.where(offset == jnp.asarray(per * at, bf16), values, zero)
            parts.append(part)
        low_row = jnp.broadcast_to(place[1:2], (TAIL, width)).astype(bf16)
        low_row = jnp.concatenate([low_row] * (LANES // TAIL), axis=0)
        return jnp.concatenate(parts, axis=0), jnp.where(lane_of == low_row, one, zero)

    def step(at, so_far):
        both = [factors(at * batch + group) for group in range(batch)]
        spread = jnp.concatenate([pair[0] for pair in both], axis=1)
        mask = jnp.concatenate([pair[1] for pair in both], axis=1)
        return so_far + dot_nt(spread, mask)

    start = jnp.zeros((pl.cdiv(high, per) * TAIL, LANES), f32)
    assembled = lax.fori_loop(0, groups // batch, step, start)
    flat = jnp.concatenate(
        [assembled[chunk * at : chunk * (at + 1)] for at in range(high)], axis=1
    )
    top = flat.astype(bf16).astype(f32)
    both = jnp.concatenate([top, flat - top], axis=0).astype(bf16)
    copy.wait()
    result = dot_nt(both, inverse[...])
    scratch[...] = jnp.zeros(scratch.shape, f32)
    scratch[:, 0:band] = result[0:chunk] + result[chunk : 2 * chunk]
    block = scratch[...].astype(bf16)
    for group in range(groups):
        out[group] = block


def corner_kernel(recv, index_rows, worked, out, *, half, chunk):
    width = index_rows.shape[1]
    groups = recv.shape[0]
    group_row = index_rows[2:3, :]
    band_row = index_rows[3:4, :]
    lane_of = lax.broadcasted_iota(jnp.int32, (LANES, width), 0).astype(f32)
    mask = jnp.where(lane_of == band_row, 1.0, 0.0).astype(bf16)
    coarse = jnp.concatenate([recv[group].astype(f32) for group in range(groups)], axis=0)
    candidate = dot_nn(coarse.astype(bf16), mask)
    which = group_row - (lax.broadcasted_iota(jnp.int32, (8, width), 0) // chunk).astype(f32)
    rows = jnp.zeros((8, width), f32)
    for at in range(0, groups * chunk, 8):
        rows = rows + jnp.where(which == float(at // chunk), candidate[at : at + 8], 0.0)
    rows = rows[0:chunk] + rows[chunk : 2 * chunk]
    block = to_tail(rows).astype(bf16)
    for peer in range(out.shape[0]):
        out[peer, 0:half, :] = worked[peer]
        out[peer, half : half + TAIL, :] = block


def take_residual(recv, tally_t, owner_map, old, half):
    subs = recv.shape[0]
    cases = old.shape[0]
    corners = jnp.concatenate(
        [
            from_tail(
                recv[peer, half : half + TAIL, :].astype(f32), cases // subs, owner_map.shape[0]
            )
            for peer in range(subs)
        ],
        axis=0,
    )
    change = collect(recv, tally_t, half) + dot_nn(corners.astype(bf16), owner_map[...])
    return old[...] - change


def residual_kernel(recv, slot_rows, owner_map, old, residual, out, *, half):
    tally_t = tally_of(slot_rows, old.shape[1])
    fresh = take_residual(recv, tally_t, owner_map, old, half)
    residual[...] = fresh
    pack(pick(fresh.astype(bf16), tally_t), out, half)


def last_kernel(recv, slot_rows, owner_map, old, residual, *, half):
    tally_t = tally_of(slot_rows, old.shape[1])
    residual[...] = take_residual(recv, tally_t, owner_map, old, half)


def body(load, visit_rows, dual_ops, dirichlet_ops, coarse_maps, primal, coarse_inverse):
    slot_rows = visit_rows[0]
    cases, owned = load.shape
    slots = slot_rows.shape[0]
    coupling = coarse_maps[0]
    corners = coupling.shape[0]
    band, total_coarse = coarse_inverse.shape
    groups = total_coarse // band
    subs = lax.axis_size("sub")
    share = slots // subs
    half = share // 2
    chunk = cases // subs
    group_corners = subs * corners

    tally = (slot_rows[:, None] == jnp.arange(owned, dtype=jnp.int32)[None, :]).astype(bf16)

    def swap_sub(blocks):
        return lax.all_to_all(blocks, "sub", split_axis=0, concat_axis=0, tiled=True)

    def swap_grp(blocks):
        return lax.all_to_all(blocks, "grp", split_axis=0, concat_axis=0, tiled=True)

    (message,) = pl.pallas_call(
        functools.partial(first_kernel, half=half),
        out_shape=(jax.ShapeDtypeStruct((subs, half + TAIL, LANES), bf16),),
        in_specs=[pl.BlockSpec(memory_space=pltpu.HBM)] * 4,
        scratch_shapes=[pltpu.VMEM((TAIL, LANES), f32)]
        + [pltpu.VMEM(x.shape, x.dtype) for x in (load, visit_rows, coupling, primal)]
        + [pltpu.SemaphoreType.DMA((4,))],
        interpret=INTERPRET,
        compiler_params=pltpu.CompilerParams(vmem_limit_bytes=48 * 1024 * 1024),
    )(*(far(x) for x in (load, visit_rows, coupling, primal)))
    first = swap_sub(message)
    dirichlet_t = dirichlet_ops[0].T
    dual_t = dual_ops[0].T
    dirichlet_t, dual_t = lax.optimization_barrier((dirichlet_t, dual_t))
    square = 2 * slots * slots * cases
    packed = ((subs, half, 2 * cases), bf16)
    longer = ((subs, half + TAIL, 2 * cases), bf16)
    field = ((cases, owned), f32)

    def apply_local(arrived, matrix_t):
        kernel = functools.partial(local_kernel, half=half)
        return call(kernel, [packed], arrived, matrix_t, flops=square)[0]

    message = apply_local(first, dirichlet_t)
    setup, message = lax.optimization_barrier((first[:, half:], message))
    group_coupling = jnp.stack(
        [setup[:, :, corners * at : corners * (at + 1)] for at in range(share // TAIL)], axis=1
    ).reshape(subs, share, corners)
    owner_map = (
        lax.dot_general(
            group_coupling,
            tally.reshape(subs, share, owned),
            (((1,), (1,)), ((0,), (0,))),
            preferred_element_type=f32,
        )
        .astype(bf16)
        .reshape(group_corners, owned)
    )
    pair_rows = setup[:, 0:2, LANES - 2 * TAIL : LANES - 2 * TAIL + corners]
    pair_rows = jnp.transpose(pair_rows, (1, 0, 2)).reshape(2, group_corners)
    pair_rows = pair_rows.astype(f32)
    coarse_row = pair_rows[0] * LANES + pair_rows[1]
    group_of = jnp.floor((coarse_row + 0.5) / band)
    zero = jnp.zeros_like(coarse_row)
    index_rows = jnp.stack(
        [pair_rows[0], pair_rows[1], group_of, coarse_row - group_of * band] + [zero] * 4
    )

    owner_map, index_rows = lax.optimization_barrier((owner_map, index_rows))

    center = 0.5 * (spectrum_high + spectrum_low)
    half_width = 0.5 * (spectrum_high - spectrum_low)
    stretch = center / half_width
    weight_now = 1.0 / stretch

    keep, gain = None, center
    multipliers = residual = load
    for iteration in range(ITERS):
        arrived = swap_sub(message)
        multipliers, message = call(
            functools.partial(direction_kernel, half=half, keep=keep, gain=gain),
            [field, longer],
            arrived,
            visit_rows,
            owner_map,
            multipliers,
            flops=square,
        )
        arrived = swap_sub(message)
        (message,) = call(
            functools.partial(contrib_kernel, half=half, chunk=chunk, width=group_corners),
            [((groups, chunk // 2, (2 if iteration else 3) * group_corners), bf16)],
            *((arrived,) if iteration else (arrived, index_rows)),
        )
        contribs = swap_grp(message)
        places = places if iteration else contribs
        worked = apply_local(arrived, dual_t)
        (message,) = pl.pallas_call(
            functools.partial(coarse_kernel, chunk=chunk, batch=min(32, groups)),
            out_shape=(jax.ShapeDtypeStruct((groups, chunk, LANES), bf16),),
            in_specs=[
                pl.BlockSpec(memory_space=pltpu.VMEM),
                pl.BlockSpec(memory_space=pltpu.VMEM),
                pl.BlockSpec(memory_space=pltpu.HBM),
            ],
            scratch_shapes=[
                pltpu.VMEM((chunk, LANES), f32),
                pltpu.VMEM(coarse_inverse.shape, bf16),
                pltpu.SemaphoreType.DMA,
            ],
            interpret=INTERPRET,
            compiler_params=pltpu.CompilerParams(vmem_limit_bytes=48 * 1024 * 1024),
        )(contribs, places, far(coarse_inverse))
        coarse_all = swap_grp(message)
        (message,) = call(
            functools.partial(corner_kernel, half=half, chunk=chunk),
            [longer],
            coarse_all,
            index_rows,
            worked,
        )
        arrived = swap_sub(message)
        if iteration + 1 < ITERS:
            residual, message = call(
                functools.partial(residual_kernel, half=half),
                [field, packed],
                arrived,
                visit_rows,
                owner_map,
                residual,
                flops=square,
            )
            message = apply_local(swap_sub(message), dirichlet_t)
            weight_next = 1.0 / (2.0 * stretch - weight_now)
            keep = weight_next * weight_now
            gain = 2.0 * weight_next / half_width
            weight_now = weight_next
        else:
            (residual,) = call(
                functools.partial(last_kernel, half=half),
                [field],
                arrived,
                visit_rows,
                owner_map,
                residual,
                flops=square,
            )
    return (multipliers, residual)


def solution(mesh):
    placed = (
        P(None, ("sub", "grp")),
        P(("sub", "grp"), None),
        P(("sub", "grp"), None, None),
        P(("sub", "grp"), None, None),
        P(("sub", "grp"), None, None),
        P(("sub", "grp"), None),
        P("grp", None),
    )
    return jax.shard_map(
        body,
        mesh=mesh,
        in_specs=placed,
        out_specs=(P(None, ("sub", "grp")), P(None, ("sub", "grp"))),
        check_vma=False,
    )
```
